32 devices in a mesh: band: 2 (over y), row: 16 (over z, x, core).
Axes of the slice: x: 2, y: 2, z: 4, core: 2. Of those that a mesh axis runs over, the one named last changes fastest.
Arguments:
- coeffs: bfloat16 [2, 6144, 4096], P(None, 'row', 'band'), may hold values from -6 to 6
- rotation: bfloat16 [2, 4096, 4096], P(None, 'row', 'band'), may hold values from -0.0625 to 0.0625
Outputs:
- rotated: bfloat16 [2, 6144, 4096], P(None, 'row', 'band')
The draws below stay inside these ranges and needn't reach their ends.
All inputs are finite; a program needn't handle non-finite values.
Results may differ from the reference program's by a relative error of at most 0.0014.
Values may be sent and summed in bfloat16 or wider, within the bound.
A program may use at most 128 MiB of HBM per device.

```python
import jax
import jax.numpy as jnp
from jax import lax

NB = 4096
ROWS = 6144


def block_scale(own_key, dims, split, low, top_value):
    def one(dim, blocks):
        heights = jax.random.uniform(jax.random.fold_in(jax.random.fold_in(own_key, 6), dim), (blocks,), jnp.float32, low / len(split), top_value / len(split))
        return jnp.repeat(jnp.exp(heights), dims[dim] // blocks).reshape((-1,) + (1,) * (len(dims) - dim - 1))

    factor_of = one(*split[0])
    for cut in split[1:]:
        factor_of = factor_of * one(*cut)
    return factor_of


def gaussian(key, shape, deviation, bound, shards=(), dtype=jnp.bfloat16):
    drawn = jax.random.normal(key, shape, jnp.float32) * deviation
    if len(shards) > 0:
        drawn = block_scale(key, shape, shards, -0.22, 0.18) * drawn
    return jnp.clip(drawn, min=-bound, max=bound).astype(dtype)


def setup_inputs(seed: int = 0) -> dict:
    key_of = jax.random.split(jax.random.key(seed), 3)
    coeffs = gaussian(key_of[0], (2, ROWS, NB), 1.0, 6.0, ((1, 16), (2, 2)))
    rotation = gaussian(key_of[1], (2, NB, NB), (2 * NB) ** -0.5, 0.0625, ((1, 16), (2, 2)))
    return {"coeffs": coeffs, "rotation": rotation}


def reference(coeffs, rotation):
    real_c = coeffs[0].astype(jnp.float32)
    imag_c = coeffs[1].astype(jnp.float32)
    real_q = rotation[0].astype(jnp.float32)
    imag_q = rotation[1].astype(jnp.float32)
    high = lax.Precision.HIGHEST
    real_out = jnp.dot(real_c, real_q, precision=high, preferred_element_type=jnp.float32) - jnp.dot(imag_c, imag_q, precision=high, preferred_element_type=jnp.float32)
    imag_out = jnp.dot(real_c, imag_q, precision=high, preferred_element_type=jnp.float32) + jnp.dot(imag_c, real_q, precision=high, preferred_element_type=jnp.float32)
    return jnp.stack([real_out, imag_out]).astype(jnp.bfloat16)
```

```python
import functools

import jax
import jax.numpy as jnp
from jax import lax
from jax.experimental import pallas as pl
from jax.experimental.pallas import tpu as pltpu
from jax.sharding import PartitionSpec as P

MESH = pl.DeviceIdType.MESH
CORES = 2
SIDES = 2
CHUNK = 512
LANES = 128
TILE = 256
FORWARDS = (2, 4, 5, 8)


def kernel(lines, bands, cuts, chunk, coeffs_ref, rotation_ref, out_ref, held, whole, total, extra, staged,
           own_sem, cross_send, cross_recv, line_send, relay_send, line_recv, mate_send, mate_recv,
           pair_send, pair_recv, side_send, side_recv, band_send, band_recv, pass_send, pass_recv,
           out_send, out_recv):
    band = lax.axis_index("band")
    row = lax.axis_index("row")
    depth = rotation_ref.shape[1]
    width = coeffs_ref.shape[2]
    share = rotation_ref.shape[2] // SIDES
    layer = SIDES * CORES * depth
    pieces = len(cuts)
    last = pieces - 1
    chunks = width // chunk
    early = chunks // 2 if bands == 2 else 0
    hops = lines - 1

    line = row // (SIDES * CORES)
    side = (row // CORES) % SIDES
    core = row % CORES

    def at(z, x, c):
        return {"row": (z * SIDES + x) * CORES + c}

    flank = at(line, 1 - side, core)
    sibling = at(line, side, 1 - core)
    partners = [{"band": (band + step) % bands} for step in range(1, bands)]
    above = line < lines - 1
    below = line > 0
    ways = ((above, at(line + 1, side, core)), (below, at(line - 1, side, core)))

    near = jnp.minimum(line, lines - 1 - line)
    rise = jnp.where(2 * line < lines - 1, 1, -1)
    others = []
    for i in range(1, lines):
        step = jnp.where(i <= 2 * near, ((i + 1) // 2) * (1 if i % 2 else -1), rise * (i - near))
        other = line + step
        onward = jnp.where(step > 0, -1, 1)
        valid = jnp.logical_and(line + onward >= 0, line + onward < lines)
        target = jnp.where(valid, line + onward, line - onward)
        others.append((other, valid, at(target, side, core)))

    barrier = pltpu.get_barrier_semaphore()
    for other in [flank, sibling] + partners:
        pl.semaphore_signal(barrier, inc=1, device_id=other, device_id_type=MESH)
    for exists, other in ways:
        @pl.when(exists)
        def _(other=other):
            pl.semaphore_signal(barrier, inc=1, device_id=other, device_id_type=MESH)
    pl.semaphore_wait(barrier, 2 + len(partners) + jnp.where(above, 1, 0) + jnp.where(below, 1, 0))

    def remote(source, target, send, recv, device):
        return pltpu.make_async_remote_copy(
            src_ref=source, dst_ref=target, send_sem=send, recv_sem=recv, device_id=device, device_id_type=MESH
        )

    def rows(z, x, c):
        return pl.ds(pl.multiple_of(((z * SIDES + x) * CORES + c) * depth, depth), depth)

    def cols(s):
        return pl.ds(cuts[s][0], cuts[s][1])

    def quarter(x, s):
        return pl.ds(pl.multiple_of(x * share + cuts[s][0], LANES), cuts[s][1])

    def half(x):
        return pl.ds(pl.multiple_of(x * share, LANES), share)

    def block(s, z, rel):
        return held.at[:, rows(z, (side, 1 - side)[rel], core), cols(s)]

    def cross(s):
        return remote(rotation_ref.at[:, :, quarter(1 - side, s)], block(s, line, 0), cross_send.at[s], cross_recv.at[s], flank)

    def lift(s, rel, way):
        source = block(s, line, 1) if rel else rotation_ref.at[:, :, quarter(side, s)]
        return remote(source, block(s, line, rel), line_send.at[s, rel, way], line_recv.at[s, line, rel], ways[way][1])

    def relay(s, i, rel):
        piece = block(s, others[i][0], rel)
        return remote(piece, piece, relay_send.at[s, i, rel], line_recv.at[s, others[i][0], rel], others[i][2])

    def give(s, z, rel):
        piece = block(s, z, rel)
        return remote(piece, piece, pair_send.at[s, z, rel], pair_recv.at[s, z, rel], sibling)

    def span(j):
        return pl.ds(j * chunk, chunk)

    def beside(j):
        return remote(coeffs_ref.at[:, :, span(j)], whole.at[side, band, :, :, span(j)], side_send.at[j], side_recv.at[j], flank)

    def spread(n, j):
        return remote(coeffs_ref.at[:, :, span(j)], whole.at[side, band, :, :, span(j)], band_send.at[n, j], band_recv.at[n, j], partners[n])

    def hand(n, j):
        piece = whole.at[1 - side, band, :, :, span(j)]
        return remote(piece, piece, pass_send.at[n, j], pass_recv.at[n, j], partners[n])

    def back(s):
        return remote(staged.at[:, :, cols(s)], out_ref.at[:, :, quarter(side, s)], out_send.at[s], out_recv.at[s], flank)

    mate = remote(rotation_ref.at[:, :, half(side)], held.at[:, rows(line, side, core), :], mate_send.at[0], mate_recv.at[0], sibling)
    own = [
        pltpu.make_async_copy(rotation_ref.at[:, :, half(side)], held.at[:, rows(line, side, core), :], own_sem.at[0]),
        pltpu.make_async_copy(coeffs_ref, whole.at[side, band], own_sem.at[1]),
    ]

    def start_own(s):
        for way, (exists, _) in enumerate(ways):
            @pl.when(exists)
            def _(way=way):
                lift(s, 0, way).start()

    crossed = 0
    passed = 0

    def feed(until):
        nonlocal crossed, passed
        for kind, index in order[crossed + passed:until]:
            if kind == 0:
                cross(index).start()
                crossed += 1
            else:
                beside(index).start()
                passed += 1

    order = [(0, 0)]
    for j in range(chunks):
        order.append((1, j))
        if j % 2 == 0 and j // 2 + 1 < pieces:
            order.append((0, j // 2 + 1))
    order += [(0, s) for s in range(pieces) if (0, s) not in order]

    start_own(0)
    feed(1)
    for j in range(early):
        for n in range(bands - 1):
            spread(n, j).start()
    feed(4)
    if pieces > 1:
        start_own(1)
    mate.start()
    for copy in own:
        copy.start()
    total[...] = jnp.zeros_like(total)

    def unit(x, start, size, target, to, s):
        which = start // width
        at_k = pl.ds(pl.multiple_of(start % width, LANES), size)
        deep = pl.ds(pl.multiple_of(start, LANES), size)
        real, imag = held[0, deep, cols(s)], held[1, deep, cols(s)]
        dot = functools.partial(jnp.dot, preferred_element_type=jnp.float32)
        left_real = whole[x, which, 0, :, at_k]
        left_imag = whole[x, which, 1, :, at_k]
        target[0, :, to] += dot(left_real, real) - dot(left_imag, imag)
        target[1, :, to] += dot(left_imag, real) + dot(left_real, imag)

    every = bands * chunks
    pair = 2 if chunks % 4 == 0 else 1

    def sweep(x, first, stop, target, to, s):
        @pl.loop(first // pair, stop // pair)
        def _(u):
            unit(x, ((band * chunks + u * pair) % every) * chunk, pair * chunk, target, to, s)

    ready = set()

    def once(key, waits):
        if key not in ready:
            ready.add(key)
            for wait in waits():
                wait()

    def have_mate():
        once("mate", lambda: [mate.wait_recv, own[0].wait])

    def have_own():
        once("own", lambda: [own[1].wait] + [spread(n, j).wait_recv for n in range(bands - 1) for j in range(early)])

    def have_layer(s, i):
        if i < 0:
            have_mate()
            once((s, i), lambda: [give(s, line, 1).wait_recv])
        else:
            once((s, i), lambda: [give(s, others[i][0], rel).wait_recv for rel in range(2)])

    def have_all(s):
        for i in range(-1, hops):
            have_layer(s, i)

    def have_side():
        once("pass", lambda: [hand(n, j).wait_recv for n in range(bands - 1) for j in range(chunks)])

    def have_late(j):
        once(("late", j), lambda: [spread(n, j).wait_recv for n in range(bands - 1)])

    pending = []

    def flush():
        while pending:
            back(pending.pop()).start()

    def settle(s):
        staged[:, :, cols(s)] = extra[:, :, pl.ds(0, cuts[s][1])].astype(staged.dtype)
        pending.append(s)

    def mine(s):
        have_own()
        have_all(s)
        sweep(side, 0, chunks + early, total, cols(s), s)

    def theirs(s):
        have_own()
        have_side()
        have_all(s)
        to = pl.ds(0, cuts[s][1])
        extra[:, :, to] = jnp.zeros((2, extra.shape[1], cuts[s][1]), extra.dtype)
        sweep(1 - side, 0, every, extra, to, s)
        settle(s)

    def partial(i):
        have_own()
        have_side()
        have_layer(last, i)
        z = line if i < 0 else others[i][0]
        to = pl.ds(0, cuts[last][1])
        if i < 0:
            extra[:, :, to] = jnp.zeros((2, extra.shape[1], cuts[last][1]), extra.dtype)
        unit(1 - side, z * layer, layer, extra, to, last)

    def late(j, s):
        for n in range(1, bands):
            if n > 1 or j >= early:
                unit(side, ((band + n) % bands) * width + j * chunk, chunk, total, cols(s), s)

    work = {}

    def plan(point, job):
        work.setdefault(min(point, pieces * hops), []).append(job)

    forwards = {}
    for j in range(chunks):
        hint = FORWARDS[j] if j < len(FORWARDS) else FORWARDS[-1]
        forwards.setdefault(min(hint, pieces * hops), []).append(j)
    begin = max(0, (pieces - 2) * hops + 1)
    for s in range(last):
        plan(max((s + 1) * hops + 1, begin + s), functools.partial(theirs, s))
    for s in range(last):
        plan((s + 1) * hops + 1, functools.partial(mine, s))

    def middle():
        for j in range(early, chunks - 1):
            have_late(j)
            for s in range(last):
                late(j, s)

    plan(last * hops + 2, middle)

    forwarded = 0
    for s in range(pieces):
        cross(s).wait_recv()
        for way, (exists, _) in enumerate(ways):
            @pl.when(exists)
            def _(way=way):
                lift(s, 1, way).start()
        give(s, line, 1).start()
        for i in range(hops):
            if i == hops - 1 and s + 2 < pieces:
                start_own(s + 2)
            for rel in range(2):
                relay(s, i, rel).wait_recv()

                @pl.when(others[i][1])
                def _():
                    relay(s, i, rel).start()

                give(s, others[i][0], rel).start()
            point = s * hops + i + 1
            flush()
            for j in forwards.get(point, []):
                beside(j).wait_recv()
                for n in range(bands - 1):
                    hand(n, j).start()
                forwarded += 1
                feed(len(order) if forwarded == chunks else 4 + 3 * forwarded)
                if forwarded == chunks:
                    feed(len(order))
                    for k in range(early, chunks):
                        for n in range(bands - 1):
                            spread(n, k).start()
            for job in work.get(point, []):
                job()
                if s == last and i == 0:
                    flush()
            if s == last:
                if i == 0:
                    partial(-1)
                partial(i)

    settle(last)
    have_all(last)
    for j in range(early, chunks - 1):
        have_late(j)
        late(j, last)
    flush()
    sweep(side, 0, chunks + early, total, cols(last), last)
    for j in range(max(early, chunks - 1), chunks):
        have_late(j)
        for s in range(last):
            late(j, s)
    for j in range(max(early, chunks - 1), chunks):
        late(j, last)
    for s in range(pieces):
        out_ref[:, :, quarter(side, s)] = total[:, :, cols(s)].astype(out_ref.dtype)

    for s in range(pieces):
        back(s).wait_recv()
        back(s).wait_send()
        cross(s).wait_send()
        give(s, line, 1).wait_send()
        for rel in range(2):
            for way, (exists, _) in enumerate(ways):
                @pl.when(exists)
                def _(way=way):
                    lift(s, rel, way).wait_send()
        for i in range(hops):
            for rel in range(2):
                @pl.when(others[i][1])
                def _():
                    relay(s, i, rel).wait_send()

                give(s, others[i][0], rel).wait_send()
    mate.wait_send()
    for j in range(chunks):
        beside(j).wait_send()
        for n in range(bands - 1):
            spread(n, j).wait_send()
            hand(n, j).wait_send()


def cuts_of(share):
    cuts = []
    at = 0
    while at < share:
        size = TILE if share - at > TILE else min(LANES, share - at)
        cuts.append((at, size))
        at += size
    return cuts


def solution(mesh):
    bands, rows = mesh.shape["band"], mesh.shape["row"]
    lines = rows // (SIDES * CORES)

    def body(coeffs, rotation):
        height, width = coeffs.shape[1:]
        depth, columns = rotation.shape[1:]
        share = columns // SIDES
        cuts = cuts_of(share)
        pieces = len(cuts)
        chunk = min(CHUNK, width)
        chunks = width // chunk
        dma = pltpu.SemaphoreType.DMA
        return pl.pallas_call(
            functools.partial(kernel, lines, bands, cuts, chunk),
            out_shape=pltpu.VMEM(coeffs.shape, jnp.bfloat16),
            in_specs=[pl.BlockSpec(memory_space=pl.ANY)] * 2,
            out_specs=pl.BlockSpec(memory_space=pltpu.VMEM),
            scratch_shapes=[
                pltpu.VMEM((2, rows * depth, share), jnp.bfloat16),
                pltpu.VMEM((SIDES, bands, 2, height, width), jnp.bfloat16),
                pltpu.VMEM((2, height, share), jnp.float32),
                pltpu.VMEM((2, height, TILE), jnp.float32),
                pltpu.VMEM((2, height, share), jnp.bfloat16),
                dma((2,)),
                dma((pieces,)),
                dma((pieces,)),
                dma((pieces, 2, 2)),
                dma((pieces, lines - 1, 2)),
                dma((pieces, lines, 2)),
                dma((1,)),
                dma((1,)),
                dma((pieces, lines, 2)),
                dma((pieces, lines, 2)),
                dma((chunks,)),
                dma((chunks,)),
                dma((bands - 1, chunks)),
                dma((bands - 1, chunks)),
                dma((bands - 1, chunks)),
                dma((bands - 1, chunks)),
                dma((pieces,)),
                dma((pieces,)),
            ],
            compiler_params=pltpu.CompilerParams(
                collective_id=0, has_side_effects=True, vmem_limit_bytes=54 * 1024 * 1024
            ),
        )(coeffs, rotation)

    in_specs = (P(None, "row", "band"), P(None, "row", "band"))
    out_specs = P(None, "row", "band")
    return jax.shard_map(body, mesh=mesh, in_specs=in_specs, out_specs=out_specs, check_vma=False)
```

```python
import functools

import jax
import jax.numpy as jnp
from jax import lax
from jax.experimental import pallas as pl
from jax.experimental.pallas import tpu as pltpu
from jax.sharding import PartitionSpec as P

MESH = pl.DeviceIdType.MESH
CORES = 2
SIDES = 2
CHUNK = 512
LANES = 128
TILE = 256

FORWARDS = ((0, 2, 1), (1, 1, 1), (1, 2, 1), (2, 1, 1))

JOBS = {
    (1, 1, 1): ((0, 0, 6, 0, 1, False), (1, 0, 2, 0, 1, False)),
    (2, 1, 1): ((0, 0, 6, 1, 2, False),),
    (2, 2, 0): ((1, 0, 2, 1, 2, False), (1, 2, 4, 0, 2, False)),
    (2, 2, 1): ((1, 4, 6, 0, 2, False),),
    (3, 1, 0): ((1, 6, 8, 0, 2, True), (1, 0, 8, 2, 3, True)),
    (3, 3, 0): ((0, 0, 6, 2, 3, False),),
    (4, 1, 0): ((1, 0, 8, 3, 4, True),),
    (4, 1, 1): ((0, 0, 6, 3, 4, False),),
    (4, 2, 0): ((0, 6, 7, 0, 4, False),),
}


def kernel(lines, bands, cuts, chunk, coeffs_ref, rotation_ref, out_ref, held, whole, total, staged,
           own_sem, cross_send, cross_recv, line_send, relay_send, line_recv, mate_send, mate_recv,
           pair_send, pair_recv, side_send, side_recv, band_send, band_recv, pass_send, pass_recv,
           out_send, out_recv):
    band = lax.axis_index("band")
    row = lax.axis_index("row")
    depth = rotation_ref.shape[1]
    width = coeffs_ref.shape[2]
    share = rotation_ref.shape[2] // SIDES
    layer = SIDES * CORES * depth
    pieces = len(cuts)
    last = pieces - 1
    chunks = width // chunk
    early = chunks // 2 if bands == 2 else 0
    hops = lines - 1

    line = row // (SIDES * CORES)
    side = (row // CORES) % SIDES
    core = row % CORES

    def at(z, x, c):
        return {"row": (z * SIDES + x) * CORES + c}

    flank = at(line, 1 - side, core)
    sibling = at(line, side, 1 - core)
    partners = [{"band": (band + step) % bands} for step in range(1, bands)]
    above = line < lines - 1
    below = line > 0
    ways = ((above, at(line + 1, side, core)), (below, at(line - 1, side, core)))

    near = jnp.minimum(line, lines - 1 - line)
    rise = jnp.where(2 * line < lines - 1, 1, -1)
    others = []
    for i in range(1, lines):
        step = jnp.where(i <= 2 * near, ((i + 1) // 2) * (1 if i % 2 else -1), rise * (i - near))
        other = line + step
        onward = jnp.where(step > 0, -1, 1)
        valid = jnp.logical_and(line + onward >= 0, line + onward < lines)
        target = jnp.where(valid, line + onward, line - onward)
        others.append((other, valid, at(target, side, core)))

    barrier = pltpu.get_barrier_semaphore()
    for other in [flank, sibling] + partners:
        pl.semaphore_signal(barrier, inc=1, device_id=other, device_id_type=MESH)
    for exists, other in ways:
        @pl.when(exists)
        def _(other=other):
            pl.semaphore_signal(barrier, inc=1, device_id=other, device_id_type=MESH)
    pl.semaphore_wait(barrier, 2 + len(partners) + jnp.where(above, 1, 0) + jnp.where(below, 1, 0))

    def remote(source, target, send, recv, device):
        return pltpu.make_async_remote_copy(
            src_ref=source, dst_ref=target, send_sem=send, recv_sem=recv, device_id=device, device_id_type=MESH
        )

    def rows(z, x, c):
        return pl.ds(pl.multiple_of(((z * SIDES + x) * CORES + c) * depth, depth), depth)

    def cols(s):
        return pl.ds(cuts[s][0], cuts[s][1])

    def quarter(x, s):
        return pl.ds(pl.multiple_of(x * share + cuts[s][0], LANES), cuts[s][1])

    def half(x):
        return pl.ds(pl.multiple_of(x * share, LANES), share)

    def block(s, z, rel):
        return held.at[:, rows(z, (side, 1 - side)[rel], core), cols(s)]

    def cross(s):
        return remote(rotation_ref.at[:, :, quarter(1 - side, s)], block(s, line, 0), cross_send.at[s], cross_recv.at[s], flank)

    def lift(s, rel, way):
        source = block(s, line, 1) if rel else rotation_ref.at[:, :, quarter(side, s)]
        return remote(source, block(s, line, rel), line_send.at[s, rel, way], line_recv.at[s, line, rel], ways[way][1])

    def relay(s, i, rel):
        piece = block(s, others[i][0], rel)
        return remote(piece, piece, relay_send.at[s, i, rel], line_recv.at[s, others[i][0], rel], others[i][2])

    def give(s, z, rel):
        piece = block(s, z, rel)
        return remote(piece, piece, pair_send.at[s, z, rel], pair_recv.at[s, z, rel], sibling)

    def span(j):
        return pl.ds(j * chunk, chunk)

    def beside(j):
        return remote(coeffs_ref.at[:, :, span(j)], whole.at[side, band, :, :, span(j)], side_send.at[j], side_recv.at[j], flank)

    def spread(n, j):
        return remote(coeffs_ref.at[:, :, span(j)], whole.at[side, band, :, :, span(j)], band_send.at[n, j], band_recv.at[n, j], partners[n])

    def hand(n, j):
        piece = whole.at[1 - side, band, :, :, span(j)]
        return remote(piece, piece, pass_send.at[n, j], pass_recv.at[n, j], partners[n])

    def back(s):
        return remote(staged.at[:, :, cols(s)], out_ref.at[:, :, quarter(side, s)], out_send.at[s], out_recv.at[s], flank)

    mate = remote(rotation_ref.at[:, :, half(side)], held.at[:, rows(line, side, core), :], mate_send.at[0], mate_recv.at[0], sibling)
    own = [
        pltpu.make_async_copy(rotation_ref.at[:, :, half(side)], held.at[:, rows(line, side, core), :], own_sem.at[0]),
        pltpu.make_async_copy(coeffs_ref, whole.at[side, band], own_sem.at[1]),
    ]

    def start_own(s):
        for way, (exists, _) in enumerate(ways):
            @pl.when(exists)
            def _(way=way):
                lift(s, 0, way).start()

    crossed = 0
    passed = 0

    def feed(until):
        nonlocal crossed, passed
        for kind, index in order[crossed + passed:until]:
            if kind == 0:
                cross(index).start()
                crossed += 1
            else:
                beside(index).start()
                passed += 1

    order = [(0, 0)]
    for j in range(chunks):
        order.append((1, j))
        if j % 2 == 0 and j // 2 + 1 < pieces:
            order.append((0, j // 2 + 1))
    order += [(0, s) for s in range(pieces) if (0, s) not in order]

    start_own(0)
    feed(1)
    for j in range(early):
        for n in range(bands - 1):
            spread(n, j).start()
    feed(4)
    if pieces > 1:
        start_own(1)
    mate.start()
    for copy in own:
        copy.start()
    total[...] = jnp.zeros_like(total)

    every = bands * chunks
    pair = 2 if chunks % 2 == 0 else 1
    ready = set()
    left = {(rel, s): set(range(every)) for rel in range(2) for s in range(pieces)}

    def once(key, waits):
        if key not in ready:
            ready.add(key)
            for copy, action in waits():
                getattr(copy, action)()

    def have_coeffs(rel, u):
        n, j = u // chunks, u % chunks
        if n == 0 and rel == 0:
            once("own", lambda: [(own[1], "wait")])
        elif rel == 0:
            once((0, u), lambda: [(spread(n - 1, j), "wait_recv")])
        elif n > 0:
            once((1, u), lambda: [(hand(n - 1, j), "wait_recv")])

    def have_layer(s, i):
        if i < 0:
            once("mate", lambda: [(mate, "wait_recv"), (own[0], "wait")])
            once((s, i, "layer"), lambda: [(give(s, line, 1), "wait_recv")])
        else:
            once((s, i, "layer"), lambda: [(give(s, others[i][0], rel), "wait_recv") for rel in range(2)])

    def unit(rel, start, size, to):
        x = (side, 1 - side)[rel]
        which = start // width
        at_k = pl.ds(pl.multiple_of(start % width, LANES), size)
        deep = pl.ds(pl.multiple_of(start, LANES), size)
        real, imag = held[0, deep, to], held[1, deep, to]
        dot = functools.partial(jnp.dot, preferred_element_type=jnp.float32)
        left_real = whole[x, which, 0, :, at_k]
        left_imag = whole[x, which, 1, :, at_k]
        total[rel, 0, :, to] += dot(left_real, real) - dot(left_imag, imag)
        total[rel, 1, :, to] += dot(left_imag, real) + dot(left_real, imag)

    def sweep(rel, low, high, first, stop):
        for s in range(first, stop):
            for i in range(-1, hops):
                have_layer(s, i)
            left[rel, s] -= set(range(low, high))
        for u in range(low, high):
            have_coeffs(rel, u)
        step = pair if low % pair == 0 and high % pair == 0 else 1
        count = (high - low) // step
        at, size = cuts[first]

        @pl.loop(0, count * (stop - first))
        def _(t):
            u = low + t % count * step
            to = pl.ds(pl.multiple_of(at + t // count * size, LANES), size)
            unit(rel, (band * chunks + u) % every * chunk, step * chunk, to)

    def finish(rel, s):
        run = sorted(left[rel, s])
        while run:
            n = 1
            while n < len(run) and run[n] == run[0] + n:
                n += 1
            sweep(rel, run[0], run[0] + n, s, s + 1)
            run = run[n:]

    pending = []

    def flush():
        while pending:
            back(pending.pop(0)).start()

    def settle(s):
        staged[:, :, cols(s)] = total[1, :, :, cols(s)].astype(staged.dtype)
        pending.append(s)

    def partial(i):
        for u in range(every):
            have_coeffs(1, u)
        have_layer(last, i)
        unit(1, (line if i < 0 else others[i][0]) * layer, layer, cols(last))

    def work(job):
        rel, low, high, first, stop, settled = job
        stop = min(stop, last + 1 - rel)
        high = min(high, every)
        while first < stop:
            end = first
            while end < stop and cuts[end][1] == cuts[first][1]:
                end += 1
            if set(range(low, high)) <= left[rel, first] and low < high:
                sweep(rel, low, high, first, end)
            if settled:
                for s in range(first, end):
                    finish(rel, s)
                    settle(s)
            first = end

    def enter(s):
        cross(s).wait_recv()
        for way, (exists, _) in enumerate(ways):
            @pl.when(exists)
            def _(way=way):
                lift(s, 1, way).start()
        give(s, line, 1).start()

    def arrive(s, i, rel):
        if i == hops - 1 and rel == 0 and s + 2 < pieces:
            start_own(s + 2)
        relay(s, i, rel).wait_recv()

        @pl.when(others[i][1])
        def _():
            relay(s, i, rel).start()

        give(s, others[i][0], rel).start()

    forwarded = 0
    for s in range(pieces):
        for i in range(hops):
            for rel in range(2):
                point = (s, i + 1, rel)
                if i == 0 and rel == 0:
                    enter(s)
                arrive(s, i, rel)
                flush()
                while forwarded < chunks and (FORWARDS[min(forwarded, len(FORWARDS) - 1)] <= point or s == last):
                    j = forwarded
                    beside(j).wait_recv()
                    for n in range(bands - 1):
                        hand(n, j).start()
                    forwarded += 1
                    feed(4 + 3 * forwarded)
                    if forwarded == chunks:
                        feed(len(order))
                        for k in range(early, chunks):
                            for n in range(bands - 1):
                                spread(n, k).start()
                for job in JOBS.get(point, ()):
                    work(job)
            if s == last:
                if i == 0:
                    for t in range(last):
                        if left[1, t]:
                            finish(1, t)
                            settle(t)
                    partial(-1)

    for i in range(hops):
        partial(i)

    settle(last)
    if set(range(pair)) <= left[0, last]:
        sweep(0, 0, pair, last, pieces)
    flush()
    finish(0, last)
    work((0, every - 1, every, 0, last, False))
    for s in range(last):
        finish(0, s)
    out_ref[:, :, half(side)] = total[0].astype(out_ref.dtype)

    for s in range(pieces):
        back(s).wait_recv()
        back(s).wait_send()
        cross(s).wait_send()
        give(s, line, 1).wait_send()
        for rel in range(2):
            for way, (exists, _) in enumerate(ways):
                @pl.when(exists)
                def _(way=way):
                    lift(s, rel, way).wait_send()
        for i in range(hops):
            for rel in range(2):
                @pl.when(others[i][1])
                def _():
                    relay(s, i, rel).wait_send()

                give(s, others[i][0], rel).wait_send()
    mate.wait_send()
    for j in range(chunks):
        beside(j).wait_send()
        for n in range(bands - 1):
            spread(n, j).wait_send()
            hand(n, j).wait_send()


def cuts_of(share):
    cuts = []
    at = 0
    while at < share:
        size = TILE if share - at > TILE else min(LANES, share - at)
        cuts.append((at, size))
        at += size
    return cuts


def solution(mesh):
    bands, rows = mesh.shape["band"], mesh.shape["row"]
    lines = rows // (SIDES * CORES)

    def body(coeffs, rotation):
        height, width = coeffs.shape[1:]
        depth, columns = rotation.shape[1:]
        share = columns // SIDES
        cuts = cuts_of(share)
        pieces = len(cuts)
        chunk = min(CHUNK, width)
        chunks = width // chunk
        dma = pltpu.SemaphoreType.DMA
        return pl.pallas_call(
            functools.partial(kernel, lines, bands, cuts, chunk),
            out_shape=pltpu.VMEM(coeffs.shape, jnp.bfloat16),
            in_specs=[pl.BlockSpec(memory_space=pl.ANY)] * 2,
            out_specs=pl.BlockSpec(memory_space=pltpu.VMEM),
            scratch_shapes=[
                pltpu.VMEM((2, rows * depth, share), jnp.bfloat16),
                pltpu.VMEM((SIDES, bands, 2, height, width), jnp.bfloat16),
                pltpu.VMEM((2, 2, height, share), jnp.float32),
                pltpu.VMEM((2, height, share), jnp.bfloat16),
                dma((2,)),
                dma((pieces,)),
                dma((pieces,)),
                dma((pieces, 2, 2)),
                dma((pieces, lines - 1, 2)),
                dma((pieces, lines, 2)),
                dma((1,)),
                dma((1,)),
                dma((pieces, lines, 2)),
                dma((pieces, lines, 2)),
                dma((chunks,)),
                dma((chunks,)),
                dma((bands - 1, chunks)),
                dma((bands - 1, chunks)),
                dma((bands - 1, chunks)),
                dma((bands - 1, chunks)),
                dma((pieces,)),
                dma((pieces,)),
            ],
            compiler_params=pltpu.CompilerParams(
                collective_id=0, has_side_effects=True, vmem_limit_bytes=54 * 1024 * 1024
            ),
        )(coeffs, rotation)

    in_specs = (P(None, "row", "band"), P(None, "row", "band"))
    out_specs = P(None, "row", "band")
    return jax.shard_map(body, mesh=mesh, in_specs=in_specs, out_specs=out_specs, check_vma=False)
```
